256 devices in a mesh: seq: 32 (over z, y_hi, core), tp: 8 (over y_lo, x).
Axes of the slice: x: 4, y: 4 (y_hi: 2, y_lo: 2; y = y_hi * 2 + y_lo), z: 8, core: 2. Of those that a mesh axis runs over, the one named last changes fastest.
Arguments:
- queries: bfloat16 [8192, 5120], P('seq', 'tp'), may hold values from -120 to 120, as said below
- prompt_keys: bfloat16 [4096, 1024], P('seq', 'tp'), may hold values from -4 to 4
- prompt_values: bfloat16 [4096, 1024], P('seq', 'tp'), may hold values from -6 to 6
- response_keys: bfloat16 [8192, 1024], P('seq', 'tp'), may hold values from -6 to 6
- response_values: bfloat16 [8192, 1024], P('seq', 'tp'), may hold values from -6 to 6
- lengths: int32 [16], replicated, may hold values from 1 to 4096, 8192 in all
- out_weight: bfloat16 [5120, 5120], P('tp'), may hold values from -0.125 to 0.125
Outputs:
- projected: bfloat16 [8192, 5120], P('seq', 'tp')
The draws below stay inside these ranges and needn't reach their ends.
Inputs may be any that keep to these rules, and one draw needn't show every extreme that they name: `queries`: in a few rows a query head may be a multiple of a prompt key of its key head. 16 lengths that sum to 8192; the longest has exactly 4096 tokens.
All inputs are finite; a program needn't handle non-finite values.
Results may differ from the reference program's by a relative error of at most 0.014.
Values may be sent and summed in bfloat16 or wider, within the bound.
A program may use at most 192 MiB of HBM per device.

```python
import math
import jax
import jax.numpy as jnp
import numpy as np
from jax import lax

D = 5120
HEADS = 40
KVH = 8
HD = 128
N_RESP = 16
PROMPT = 4096
RESP = 8192
MOST = 4096
N_TP = 8


def prompt_key_base(key):
    drawn = jax.random.normal(jax.random.fold_in(key, 11), (PROMPT, KVH * HD), jnp.float32)
    return jnp.clip(drawn, -4.0, 4.0)


def draw_prompt_keys(key, part):
    return prompt_key_base(key).astype(jnp.bfloat16)


def draw_queries(key, part):
    drawn = jax.random.normal(jax.random.fold_in(key, 12), (RESP, HEADS * HD), jnp.float32)
    return drawn.astype(jnp.bfloat16)


def strengthened(entries, key, source, target, shards_of, factor):
    def block_of(axis_at):
        return (jnp.arange(entries.shape[axis_at]) // (entries.shape[axis_at] // shards_of)).reshape((-1,) + (1,) * (entries.ndim - 1 - axis_at))

    first = jax.random.permutation(key, shards_of)[block_of(target)]
    far = (block_of(target) + shards_of // 2) % shards_of
    return jnp.where((block_of(source) == first) | (block_of(source) == far), factor * entries, entries)


def block_scale(stream_key, shape, shards, least, top_value):
    factor_of = 1.0
    for dim, parts in shards:
        draws = jax.random.uniform(jax.random.fold_in(jax.random.fold_in(stream_key, 6), dim), (parts,), jnp.float32, least / len(shards), top_value / len(shards))
        factor_of = factor_of * jnp.repeat(jnp.exp(draws), shape[dim] // parts).reshape((-1,) + (1,) * (len(shape) - 1 - dim))
    return factor_of


def length_profile(count, total, bound, skew):
    weights = [(1 << 20) // math.isqrt(rank ** skew) + 1 for rank in range(2, count + 1)]
    spare, holding = total - bound - (count - 1), [1] * (count - 1)
    while spare > 0:
        free = [i for i in range(count - 1) if holding[i] < bound]
        pool, remaining = sum([weights[i] for i in free]), spare
        for i in free:
            addition = min(bound - holding[i], max(1, remaining * weights[i] // pool), spare)
            holding[i] = holding[i] + addition
            spare = spare - addition
    return np.array([bound] + holding)


def ragged_sizes(rng, amount, total, reach, skew):
    if amount == 2:
        one = jax.random.randint(rng, (), max(1, total - reach), min(reach, total - 1) + 1)
        return jnp.stack([one, total - one])
    sizes = jnp.asarray(length_profile(amount, total, reach, skew), jnp.int32)
    couples = (amount - 1) // 2
    source_of, taker = sizes[1:1 + 2 * couples:2], sizes[2:2 + 2 * couples:2]
    slack = jnp.minimum(source_of - 1, reach - taker)
    shifted = jax.random.randint(jax.random.fold_in(rng, 1), (couples,), 0, 1 << 20) % (slack + 1)
    sizes = sizes.at[1:1 + 2 * couples:2].set(source_of - shifted).at[2:2 + 2 * couples:2].set(taker + shifted)
    return sizes[jax.random.permutation(jax.random.fold_in(rng, 2), amount)]


def normal_values(own_key, shape, width, most, split=(), held_as=jnp.bfloat16):
    loudness = block_scale(own_key, shape, split, -0.22, 0.18) if split else 1.0
    values = jax.random.normal(own_key, shape, jnp.float32) * width * loudness
    return jnp.minimum(jnp.maximum(values, -most), most).astype(held_as)


def heavy_noise(key, shape, deviation, limit, cuts, heavy, held_as=jnp.bfloat16):
    result = deviation * jax.random.normal(key, shape, jnp.float32)
    if cuts:
        result = result * block_scale(key, shape, cuts, -0.22, 0.18)
    return jnp.clip(strengthened(result, jax.random.fold_in(key, 3), *heavy), -limit, limit).astype(held_as)


def setup_inputs(seed: int = 0) -> dict:
    keys = jax.random.split(jax.random.key(seed), 8)
    queries = draw_queries(jax.random.fold_in(keys[7], 71), 0)
    prompt_keys = draw_prompt_keys(jax.random.fold_in(keys[7], 71), 0)
    prompt_values = normal_values(keys[2], (PROMPT, KVH * HD), 1.0, 6.0, ((0, 32), (1, 8)))
    response_keys = normal_values(keys[3], (RESP, KVH * HD), 1.0, 6.0, ((0, 32), (1, 8)))
    response_values = normal_values(keys[4], (RESP, KVH * HD), 1.0, 6.0, ((0, 32), (1, 8)))
    lengths = ragged_sizes(keys[5], N_RESP, RESP, MOST, 2).astype(jnp.int32)
    out_weight = heavy_noise(keys[6], (HEADS * HD, D), (HEADS * HD) ** -0.5, 0.125, ((0, 8),), (0, 1, 8, 2.0))
    return dict(queries=queries, prompt_keys=prompt_keys, prompt_values=prompt_values, response_keys=response_keys, response_values=response_values, lengths=lengths, out_weight=out_weight)


def segment_layout(lengths):
    positions = jnp.arange(RESP, dtype=jnp.int32)
    seg_ends = jnp.cumsum(lengths).astype(jnp.int32)
    seg_starts = seg_ends - lengths
    inside = (positions[:, None] >= seg_starts[None, :]) & (positions[:, None] < seg_ends[None, :])
    own_start = jnp.sum(jnp.where(inside, seg_starts[None, :], 0), axis=1).astype(jnp.int32)
    return positions, own_start


def reference(queries, prompt_keys, prompt_values, response_keys, response_values, lengths, out_weight):
    group_size = HEADS // KVH
    block_rows = math.gcd(RESP, 128)
    window = min(MOST + block_rows, RESP)
    scale_factor = HD ** -0.5
    positions, own_start = segment_layout(lengths)
    prompt_k = prompt_keys.astype(jnp.float32).reshape(PROMPT, KVH, HD)
    prompt_v = prompt_values.astype(jnp.float32).reshape(PROMPT, KVH, HD)

    def one_block(index):
        first_row = (index * block_rows).astype(jnp.int32)
        query_block = lax.dynamic_slice_in_dim(queries, first_row, block_rows, 0)
        query_block = query_block.astype(jnp.float32).reshape(block_rows, KVH, group_size, HD)
        query_pos = lax.dynamic_slice_in_dim(positions, first_row, block_rows, 0)
        query_first = lax.dynamic_slice_in_dim(own_start, first_row, block_rows, 0)
        begin = jnp.clip(first_row + block_rows - window, 0, RESP - window).astype(jnp.int32)
        resp_k = lax.dynamic_slice_in_dim(response_keys, begin, window, 0).astype(jnp.float32).reshape(window, KVH, HD)
        resp_v = lax.dynamic_slice_in_dim(response_values, begin, window, 0).astype(jnp.float32).reshape(window, KVH, HD)
        key_pos = begin + jnp.arange(window, dtype=jnp.int32)
        visible = (key_pos[None, :] <= query_pos[:, None]) & (key_pos[None, :] >= query_first[:, None])
        prompt_scores = jnp.einsum("rkgd,nkd->rkgn", query_block, prompt_k) * scale_factor
        resp_scores = jnp.einsum("rkgd,nkd->rkgn", query_block, resp_k) * scale_factor
        resp_scores = jnp.where(visible[:, None, None, :], resp_scores, -jnp.inf)
        scores = jnp.concatenate([prompt_scores, resp_scores], axis=3)
        top = jnp.max(scores, axis=3)
        weights = jnp.exp(scores - top[..., None])
        summed = jnp.sum(weights, axis=3)
        rounded = lax.optimization_barrier(weights.astype(jnp.bfloat16)).astype(jnp.float32)
        all_values = jnp.concatenate([prompt_v, resp_v], axis=0)
        numer = jnp.einsum("rkgn,nkd->rkgd", rounded, all_values)
        return (numer / summed[..., None]).astype(jnp.bfloat16).reshape(block_rows, HEADS * HD)

    attended = lax.map(one_block, jnp.arange(RESP // block_rows, dtype=jnp.int32))
    attended = attended.reshape(RESP, HEADS * HD)
    group_cols = HEADS * HD // N_TP
    total = jnp.zeros((RESP, D), jnp.float32)
    for group in range(N_TP):
        cols = attended[:, group * group_cols:(group + 1) * group_cols]
        rows = out_weight[group * group_cols:(group + 1) * group_cols, :]
        partial_term = jnp.dot(cols, rows, preferred_element_type=jnp.float32).astype(jnp.bfloat16)
        total = total + partial_term.astype(jnp.float32)
    return total.astype(jnp.bfloat16)
```

```python
import functools

import jax
import jax.numpy as jnp
from jax import lax
from jax.experimental import pallas as pl
from jax.experimental.pallas import tpu as pltpu
from jax.sharding import PartitionSpec as P

HEADS = 40
KVH = 8
HD = 128
GROUP = HEADS // KVH
N_RESP = 16
PLANES = 8
SLOTS = 32
PROWS = 128
RROWS = 256
SCALE = HD**-0.5 * 1.4426950408889634
LOW = -1e30
MESH = pl.DeviceIdType.MESH


PLAN = [
    ([(0, 1, 0), (0, -1, 0), (0, 0, 1)], 0, [(0, 0), (0, 2), (1, 0), (-1, 0), (0, 1), (1, 2), (-1, 2), (0, 3)], [[(0, 2, 0), (1, 1, 0)]]),
    ([(1, 0, 1), (0, 1, 1), (0, -2, 0), (0, -1, 1), (0, 3, 0)], 0, [(2, 0), (1, 1), (-2, 0), (2, 2), (-1, 1), (3, 0), (1, 3), (-2, 2)], [[(0, 2, 1)]]),
    ([(1, 1, 1), (1, 2, 0), (0, 4, 0)], 1, [(1, 0), (1, 2), (1, 1), (2, 0)], [[(0, -2, 1), (0, 3, 1)]]),
    ([(0, 5, 0)], 0, [(-1, 3), (3, 2), (2, 1), (2, 3), (4, 0), (-2, 1), (3, 1), (4, 2)], [[(1, 3, 0), (0, 4, 1)]]),
    ([(1, 2, 1)], 1, [(1, 3), (2, 2), (3, 0), (2, 1)], [[(0, 5, 1)]]),
    ([(1, 4, 0)], 0, [(-2, 3), (3, 3), (5, 0), (5, 2), (4, 1), (4, 3), (5, 1), (5, 3)], [[(1, 3, 1)]]),
    ([], 1, [(3, 2), (2, 3), (3, 1), (3, 3)], [[]]),
    ([(1, 4, 1)], 2, [(4, 0), (4, 1), (4, 2), (4, 3), (0, 0), (0, 1), (0, 2), (0, 3)], [[]]),
]

SPLIT = (2, 5)
DOWN, UP = 5, 2


def attend(q_ref, keys, values, bias_ref, top_ref, acc_ref, heads):
    count = keys.shape[0]
    widened = jnp.concatenate([values, jnp.ones((count, HD), jnp.bfloat16)], axis=1)
    for head in heads:
        scores = lax.dot_general(
            q_ref[:, head * HD : (head + 1) * HD],
            keys,
            (((1,), (1,)), ((), ())),
            preferred_element_type=jnp.float32,
        )
        if bias_ref is not None:
            scores = scores + bias_ref[:, :count]
        before = top_ref[head]
        top = jnp.maximum(before, jnp.max(scores, axis=1, keepdims=True) * SCALE)
        weights = jnp.exp2(scores * SCALE - top).astype(jnp.bfloat16)
        top_ref[head] = top
        acc_ref[head] = acc_ref[head] * jnp.exp2(before - top) + jnp.dot(
            weights, widened, preferred_element_type=jnp.float32
        )


def gather_attend(
    lengths_ref, q_ref, pk_ref, pv_ref, rk_ref, rv_ref, out_ref,
    pbuf, rbuf, top_ref, acc_ref, bias_ref, first_ref, load_sem, send_sem, recv_sem,
):
    s = lax.axis_index("seq")
    z, b = s // 4, s % 4
    h, c = b // 2, b % 2
    sibling = {"seq": z * 4 + h * 2 + (1 - c)}
    across = {"seq": z * 4 + (1 - h) * 2 + c}
    up = {"seq": ((z + 1) % PLANES) * 4 + b}
    down = {"seq": ((z + PLANES - 1) % PLANES) * 4 + b}
    order = [h * 2 + c, (1 - h) * 2 + c, h * 2 + (1 - c), (1 - h) * 2 + (1 - c)]

    loads = []
    for n, (src, dst) in enumerate(
        [(pk_ref, pbuf.at[s, 0]), (pv_ref, pbuf.at[s, 1]), (rk_ref, rbuf.at[s, 0]), (rv_ref, rbuf.at[s, 1])]
    ):
        loads.append(pltpu.make_async_copy(src, dst, load_sem.at[n]))
        loads[-1].start()

    barrier = pltpu.get_barrier_semaphore()
    for peer in (sibling, across, up, down):
        pl.semaphore_signal(barrier, inc=1, device_id=peer, device_id_type=MESH)

    def slot_of(kind, away, which):
        plane = (z + (PLANES - away if kind else PLANES + away)) % PLANES
        return plane * 4 + order[which]

    def copy(kind, slot, way, peer):
        buf = rbuf if kind else pbuf
        return pltpu.make_async_remote_copy(
            src_ref=buf.at[slot],
            dst_ref=buf.at[slot],
            send_sem=send_sem.at[kind, way, slot],
            recv_sem=recv_sem.at[kind, slot],
            device_id=peer,
            device_id_type=MESH,
        )

    sends = []

    def send(*what):
        sending = copy(*what)
        sending.start()
        sends.append(sending)

    def pass_on(kind, away, which):
        slot = slot_of(kind, away, which)
        if kind == 0:
            if away == 0 and which == 0:
                send(kind, slot, 2, across)
            if 0 <= away < DOWN:
                send(kind, slot, 1, down)
            if -UP < away <= 0:
                send(kind, slot, 3, up)
            send(kind, slot, 0, sibling)
        else:
            if which == 0:
                if away < 4:
                    send(kind, slot, 1, up)
                send(kind, slot, 2, across)
            send(kind, slot, 0, sibling)

    taken = {(0, 0, 0), (1, 0, 0)}

    def take(shard):
        if shard not in taken:
            taken.add(shard)
            copy(shard[0], slot_of(*shard), 0, sibling).wait_recv()
            if shard[2] < 2:
                pass_on(*shard)

    for copying in loads:
        copying.wait()
    pl.semaphore_wait(barrier, 4)
    pass_on(0, 0, 0)
    pass_on(1, 0, 0)

    position = s * RROWS + lax.broadcasted_iota(jnp.int32, (RROWS, 1), 0)
    first = jnp.zeros((RROWS, 1), jnp.int32)
    start = jnp.int32(0)
    for r in range(N_RESP):
        first = jnp.where(position >= start, start, first)
        start = start + lengths_ref[r]
    first_ref[...] = first
    top_ref[...] = jnp.full_like(top_ref, LOW)
    acc_ref[...] = jnp.zeros_like(acc_ref)

    def visible(slot, at):
        position = s * RROWS + lax.broadcasted_iota(jnp.int32, (RROWS, 1), 0)
        key = slot * RROWS + lax.broadcasted_iota(jnp.int32, (RROWS, RROWS), 1)
        seen = (key >= first_ref[...]) & (key <= position)
        bias_ref[:, at * RROWS : (at + 1) * RROWS] = jnp.where(seen, 0.0, LOW)

    for before, kind, shards, between in PLAN:
        for shard in before:
            take(shard)
        for away, which in shards:
            take((min(kind, 1), away, which))
        if kind < 2:
            chosen = [slot_of(kind, *shard) for shard in shards]
        else:
            chosen = []
            for i in range(5):
                own = jnp.where(i <= b, 1, 0)
                below = (z + PLANES - 4) % PLANES
                chosen.append(own * (4 * z + min(i, 3)) + (1 - own) * (4 * below + max(i - 1, 0)))
        buf = rbuf if kind else pbuf
        if kind:
            for n, slot in enumerate(chosen):
                visible(slot, n)
        keys, values = [jnp.concatenate([buf[slot, n] for slot in chosen], axis=0) for n in range(2)]
        edges = (0,) + SPLIT
        for n in range(len(SPLIT)):
            attend(q_ref, keys, values, bias_ref if kind else None, top_ref, acc_ref, range(edges[n], edges[n + 1]))
            if n < len(between):
                for shard in between[n]:
                    take(shard)

    for head in range(GROUP):
        acc = acc_ref[head]
        out_ref[:, head * HD : (head + 1) * HD] = (acc[:, :HD] / acc[:, HD:]).astype(jnp.bfloat16)

    for sending in sends:
        sending.wait_send()


def per_device(queries, prompt_keys, prompt_values, response_keys, response_values, lengths, out_weight):
    vmem = pl.BlockSpec(memory_space=pltpu.VMEM)
    attended = pl.pallas_call(
        gather_attend,
        out_shape=jax.ShapeDtypeStruct(queries.shape, jnp.bfloat16),
        in_specs=[pl.BlockSpec(memory_space=pltpu.SMEM), vmem] + [pl.BlockSpec(memory_space=pl.ANY)] * 4,
        out_specs=vmem,
        scratch_shapes=[
            pltpu.VMEM((SLOTS, 2, PROWS, HD), jnp.bfloat16),
            pltpu.VMEM((SLOTS, 2, RROWS, HD), jnp.bfloat16),
            pltpu.VMEM((GROUP, RROWS, 1), jnp.float32),
            pltpu.VMEM((GROUP, RROWS, 2 * HD), jnp.float32),
            pltpu.VMEM((RROWS, 5 * RROWS), jnp.float32),
            pltpu.VMEM((RROWS, 1), jnp.int32),
            pltpu.SemaphoreType.DMA((4,)),
            pltpu.SemaphoreType.DMA((2, 4, SLOTS)),
            pltpu.SemaphoreType.DMA((2, SLOTS)),
        ],
        compiler_params=pltpu.CompilerParams(
            collective_id=0, has_side_effects=True, vmem_limit_bytes=60 * 2**20
        ),
        name="gather_attend",
    )(lengths, queries, prompt_keys, prompt_values, response_keys, response_values)
    partial_out = jnp.dot(attended, out_weight, preferred_element_type=jnp.float32)
    return lax.psum_scatter(partial_out.astype(jnp.bfloat16), "tp", scatter_dimension=1, tiled=True)


def solution(mesh):
    in_specs = (P("seq", "tp"), P("seq", "tp"), P("seq", "tp"), P("seq", "tp"), P("seq", "tp"), P(), P("tp", None))
    return jax.shard_map(
        per_device, mesh=mesh, in_specs=in_specs, out_specs=P("seq", "tp"), check_vma=False
    )
```

```python
import functools

import jax
import jax.numpy as jnp
from jax import lax
from jax.experimental import pallas as pl
from jax.experimental.pallas import tpu as pltpu
from jax.sharding import PartitionSpec as P

HEADS = 40
KVH = 8
HD = 128
GROUP = HEADS // KVH
N_RESP = 16
PLANES = 8
SLOTS = 32
PROWS = 128
RROWS = 256
SCALE = HD**-0.5 * 1.4426950408889634
LOW = -1e30
XS = 4
COLS = 640
RA = 128
RB = RROWS - RA
ROLES = [(1, 2), (0, 2), (1, 1), (1, 3), (0, 1), (0, 3), (1, 0), (0, 0)]
MESH = pl.DeviceIdType.MESH


PLAN = [
    ([(0, 1, 0), (0, -1, 0), (0, 0, 1)], 0, [(0, 0), (0, 2), (1, 0), (-1, 0), (0, 1), (1, 2), (-1, 2), (0, 3)], [[(0, 2, 0), (1, 1, 0)]]),
    ([(1, 0, 1), (0, 1, 1), (0, -2, 0), (0, -1, 1), (0, 3, 0)], 0, [(2, 0), (1, 1), (-2, 0), (2, 2), (-1, 1), (3, 0), (1, 3), (-2, 2)], [[(0, 2, 1)]]),
    ([(1, 1, 1), (1, 2, 0), (0, 4, 0)], 1, [(1, 0), (1, 2), (1, 1), (2, 0)], [[(0, -2, 1), (0, 3, 1)]]),
    ([(0, 5, 0)], 0, [(-1, 3), (3, 2), (2, 1), (2, 3), (4, 0), (-2, 1), (3, 1), (4, 2)], [[(1, 3, 0), (0, 4, 1)]]),
    ([(1, 2, 1)], 1, [(1, 3), (2, 2), (3, 0), (2, 1)], [[(0, 5, 1)]]),
    ([(1, 4, 0)], 0, [(-2, 3), (3, 3), (5, 0), (5, 2), (4, 1), (4, 3), (5, 1), (5, 3)], [[(1, 3, 1)]]),
    ([], 1, [(3, 2), (2, 3), (3, 1), (3, 3)], [[]]),
    ([(1, 4, 1)], 2, [(4, 0), (4, 1), (4, 2), (4, 3), (0, 0), (0, 1), (0, 2), (0, 3)], [[]]),
]

SPLIT = (2, 5)
DOWN, UP = 5, 2


def attend(q_ref, keys, values, bias_ref, top_ref, acc_ref, heads):
    count = keys.shape[0]
    widened = jnp.concatenate([values, jnp.ones((count, HD), jnp.bfloat16)], axis=1)
    for head in heads:
        scores = lax.dot_general(
            q_ref[:, head * HD : (head + 1) * HD],
            keys,
            (((1,), (1,)), ((), ())),
            preferred_element_type=jnp.float32,
        )
        if bias_ref is not None:
            scores = scores + bias_ref[:, :count]
        before = top_ref[head]
        top = jnp.maximum(before, jnp.max(scores, axis=1, keepdims=True) * SCALE)
        weights = jnp.exp2(scores * SCALE - top).astype(jnp.bfloat16)
        top_ref[head] = top
        acc_ref[head] = acc_ref[head] * jnp.exp2(before - top) + jnp.dot(
            weights, widened, preferred_element_type=jnp.float32
        )


def attention_block(
    lengths_ref, q_ref, pk_ref, pv_ref, rk_ref, rv_ref, w_ref, out_ref,
    pbuf, rbuf, top_ref, acc_ref, bias_ref, first_ref, wbuf, att_ref, part,
    from_y, from_y_late, step1, step2, late1, late2,
    load_sem, send_sem, recv_sem, psend_sem, precv_sem,
):
    s = lax.axis_index("seq")
    z, b = s // 4, s % 4
    h, c = b // 2, b % 2
    sibling = {"seq": z * 4 + h * 2 + (1 - c)}
    across = {"seq": z * 4 + (1 - h) * 2 + c}
    up = {"seq": ((z + 1) % PLANES) * 4 + b}
    down = {"seq": ((z + PLANES - 1) % PLANES) * 4 + b}
    t = lax.axis_index("tp")
    yl, x = t // XS, t % XS
    right = {"tp": yl * XS + (x + 1) % XS}
    left = {"tp": yl * XS + (x + XS - 1) % XS}
    beside = {"tp": (1 - yl) * XS + x}
    order = [h * 2 + c, (1 - h) * 2 + c, h * 2 + (1 - c), (1 - h) * 2 + (1 - c)]

    loads = []
    for n, (src, dst) in enumerate(
        [
            (pk_ref, pbuf.at[s, 0]),
            (pv_ref, pbuf.at[s, 1]),
            (rk_ref, rbuf.at[s, 0]),
            (rv_ref, rbuf.at[s, 1]),
            (w_ref, wbuf),
        ]
    ):
        loads.append(pltpu.make_async_copy(src, dst, load_sem.at[n]))
        loads[-1].start()

    barrier = pltpu.get_barrier_semaphore()
    for peer in (sibling, across, up, down, right, left, beside):
        pl.semaphore_signal(barrier, inc=1, device_id=peer, device_id_type=MESH)

    def slot_of(kind, away, which):
        plane = (z + (PLANES - away if kind else PLANES + away)) % PLANES
        return plane * 4 + order[which]

    def copy(kind, slot, way, peer):
        buf = rbuf if kind else pbuf
        return pltpu.make_async_remote_copy(
            src_ref=buf.at[slot],
            dst_ref=buf.at[slot],
            send_sem=send_sem.at[kind, way, slot],
            recv_sem=recv_sem.at[kind, slot],
            device_id=peer,
            device_id_type=MESH,
        )

    sends = []

    def send(*what):
        sending = copy(*what)
        sending.start()
        sends.append(sending)

    def pass_on(kind, away, which):
        slot = slot_of(kind, away, which)
        if kind == 0:
            if away == 0 and which == 0:
                send(kind, slot, 2, across)
            if 0 <= away < DOWN:
                send(kind, slot, 1, down)
            if -UP < away <= 0:
                send(kind, slot, 3, up)
            send(kind, slot, 0, sibling)
        else:
            if which == 0:
                if away < 4:
                    send(kind, slot, 1, up)
                send(kind, slot, 2, across)
            send(kind, slot, 0, sibling)

    taken = {(0, 0, 0), (1, 0, 0)}

    def take(shard):
        if shard not in taken:
            taken.add(shard)
            copy(shard[0], slot_of(*shard), 0, sibling).wait_recv()
            if shard[2] < 2:
                pass_on(*shard)

    for copying in loads[:4]:
        copying.wait()
    pl.semaphore_wait(barrier, 7)
    pass_on(0, 0, 0)
    pass_on(1, 0, 0)

    position = s * RROWS + lax.broadcasted_iota(jnp.int32, (RROWS, 1), 0)
    first = jnp.zeros((RROWS, 1), jnp.int32)
    start = jnp.int32(0)
    for r in range(N_RESP):
        first = jnp.where(position >= start, start, first)
        start = start + lengths_ref[r]
    first_ref[...] = first
    top_ref[...] = jnp.full_like(top_ref, LOW)
    acc_ref[...] = jnp.zeros_like(acc_ref)

    def visible(slot, at):
        position = s * RROWS + lax.broadcasted_iota(jnp.int32, (RROWS, 1), 0)
        key = slot * RROWS + lax.broadcasted_iota(jnp.int32, (RROWS, RROWS), 1)
        seen = (key >= first_ref[...]) & (key <= position)
        bias_ref[:, at * RROWS : (at + 1) * RROWS] = jnp.where(seen, 0.0, LOW)

    for before, kind, shards, between in PLAN:
        for shard in before:
            take(shard)
        for away, which in shards:
            take((min(kind, 1), away, which))
        if kind < 2:
            chosen = [slot_of(kind, *shard) for shard in shards]
        else:
            chosen = []
            for i in range(5):
                own = jnp.where(i <= b, 1, 0)
                below = (z + PLANES - 4) % PLANES
                chosen.append(own * (4 * z + min(i, 3)) + (1 - own) * (4 * below + max(i - 1, 0)))
        buf = rbuf if kind else pbuf
        if kind:
            for n, slot in enumerate(chosen):
                visible(slot, n)
        keys, values = [jnp.concatenate([buf[slot, n] for slot in chosen], axis=0) for n in range(2)]
        edges = (0,) + SPLIT
        for n in range(len(SPLIT)):
            attend(q_ref, keys, values, bias_ref if kind else None, top_ref, acc_ref, range(edges[n], edges[n + 1]))
            if n < len(between):
                for shard in between[n]:
                    take(shard)

    for head in range(GROUP):
        acc = acc_ref[head]
        att_ref[:, head * HD : (head + 1) * HD] = (acc[:, :HD] / acc[:, HD:]).astype(jnp.bfloat16)

    loads[4].wait()
    count = 0

    def hand(src, dst, peer):
        nonlocal count
        sending = pltpu.make_async_remote_copy(
            src_ref=src,
            dst_ref=dst,
            send_sem=psend_sem.at[count],
            recv_sem=precv_sem.at[count],
            device_id=peer,
            device_id_type=MESH,
        )
        count += 1
        sending.start()
        sends.append(sending)
        return sending

    def compute(role):
        other, dx = ROLES[role]
        target = ((1 - yl) if other else yl) * XS + (x + dx) % XS
        columns = pl.ds(pl.multiple_of(target * COLS, HD), COLS)
        part[role] = jnp.dot(att_ref[...], wbuf[:, columns], preferred_element_type=jnp.float32).astype(jnp.bfloat16)

    def add(role, rows, *others):
        total = part[role, rows].astype(jnp.float32)
        for other in others:
            total = total + other.astype(jnp.float32)
        part[role, rows] = total.astype(jnp.bfloat16)

    rows_a, rows_b = slice(0, RA), slice(RA, RROWS)
    high_a, low_a = slice(0, RA // 2), slice(RA // 2, RA)
    high_b, low_b = slice(RA, RA + RB // 2), slice(RA + RB // 2, RROWS)
    ya, b1, b2 = {}, {}, {}
    compute(0)
    ya[0] = hand(part.at[0, rows_a], from_y.at[0], beside)
    b1[0, 0] = hand(part.at[0, high_b], step1.at[0, 0], right)
    b1[1, 0] = hand(part.at[0, low_b], step1.at[1, 0], left)
    compute(1)
    b1[0, 1] = hand(part.at[1, high_b], step1.at[0, 1], right)
    b1[1, 1] = hand(part.at[1, low_b], step1.at[1, 1], left)
    compute(2)
    ya[1] = hand(part.at[2, rows_a], from_y.at[1], beside)
    compute(3)
    ya[2] = hand(part.at[3, rows_a], from_y.at[2], beside)
    compute(6)
    ya[3] = hand(part.at[6, rows_a], from_y.at[3], beside)
    compute(4)
    compute(5)
    ya[0].wait_recv()
    add(1, rows_a, from_y[0])
    a1 = [hand(part.at[1, high_a], late1.at[0], right), hand(part.at[1, low_a], late1.at[1], left)]
    for n, (to_right, to_left) in enumerate([(2, 3), (4, 5)]):
        b1[0, n].wait_recv()
        add(to_right, high_b, step1[0, n])
        b2[0, n] = hand(part.at[to_right, rows_b], step2.at[0, n], right)
        b1[1, n].wait_recv()
        add(to_left, low_b, step1[1, n])
        b2[1, n] = hand(part.at[to_left, rows_b], step2.at[1, n], left)
    compute(7)
    a2 = []
    for n in range(2):
        ya[1 + n].wait_recv()
        add(4 + n, rows_a, from_y[1 + n])
        a1[n].wait_recv()
        add(4 + n, low_a if n else high_a, late1[n])
        a2.append(hand(part.at[4 + n, rows_a], late2.at[n], left if n else right))
    for n in range(2):
        b2[n, 0].wait_recv()
    add(6, rows_b, step2[0, 0], step2[1, 0])
    yb = hand(part.at[6, rows_b], from_y_late, beside)
    ya[3].wait_recv()
    for n in range(2):
        a2[n].wait_recv()

    def total(rows, *others):
        result = part[7, rows].astype(jnp.float32)
        for other in others:
            result = result + other.astype(jnp.float32)
        out_ref[rows, :] = result.astype(jnp.bfloat16)

    total(rows_a, from_y[3], late2[0], late2[1])
    for n in range(2):
        b2[n, 1].wait_recv()
    yb.wait_recv()
    total(rows_b, step2[0, 1], step2[1, 1], from_y_late[...])

    for sending in sends:
        sending.wait_send()


def per_device(queries, prompt_keys, prompt_values, response_keys, response_values, lengths, out_weight):
    vmem = pl.BlockSpec(memory_space=pltpu.VMEM)
    return pl.pallas_call(
        attention_block,
        out_shape=jax.ShapeDtypeStruct((RROWS, COLS), jnp.bfloat16),
        in_specs=[pl.BlockSpec(memory_space=pltpu.SMEM), vmem] + [pl.BlockSpec(memory_space=pl.ANY)] * 5,
        out_specs=vmem,
        scratch_shapes=[
            pltpu.VMEM((SLOTS, 2, PROWS, HD), jnp.bfloat16),
            pltpu.VMEM((SLOTS, 2, RROWS, HD), jnp.bfloat16),
            pltpu.VMEM((GROUP, RROWS, 1), jnp.float32),
            pltpu.VMEM((GROUP, RROWS, 2 * HD), jnp.float32),
            pltpu.VMEM((RROWS, 5 * RROWS), jnp.float32),
            pltpu.VMEM((RROWS, 1), jnp.int32),
            pltpu.VMEM(out_weight.shape, jnp.bfloat16),
            pltpu.VMEM((RROWS, GROUP * HD), jnp.bfloat16),
            pltpu.VMEM((8, RROWS, COLS), jnp.bfloat16),
            pltpu.VMEM((4, RA, COLS), jnp.bfloat16),
            pltpu.VMEM((RB, COLS), jnp.bfloat16),
            pltpu.VMEM((2, 2, RB // 2, COLS), jnp.bfloat16),
            pltpu.VMEM((2, 2, RB, COLS), jnp.bfloat16),
            pltpu.VMEM((2, RA // 2, COLS), jnp.bfloat16),
            pltpu.VMEM((2, RA, COLS), jnp.bfloat16),
            pltpu.SemaphoreType.DMA((5,)),
            pltpu.SemaphoreType.DMA((2, 4, SLOTS)),
            pltpu.SemaphoreType.DMA((2, SLOTS)),
            pltpu.SemaphoreType.DMA((17,)),
            pltpu.SemaphoreType.DMA((17,)),
        ],
        compiler_params=pltpu.CompilerParams(
            collective_id=0, has_side_effects=True, vmem_limit_bytes=60 * 2**20
        ),
        name="attention_block",
    )(lengths, queries, prompt_keys, prompt_values, response_keys, response_values, out_weight)


def solution(mesh):
    in_specs = (P("seq", "tp"), P("seq", "tp"), P("seq", "tp"), P("seq", "tp"), P("seq", "tp"), P(), P("tp", None))
    return jax.shard_map(
        per_device, mesh=mesh, in_specs=in_specs, out_specs=P("seq", "tp"), check_vma=False
    )
```

```python
import functools

import jax
import jax.numpy as jnp
from jax import lax
from jax.experimental import pallas as pl
from jax.experimental.pallas import tpu as pltpu
from jax.sharding import PartitionSpec as P

HEADS = 40
KVH = 8
HD = 128
GROUP = HEADS // KVH
N_RESP = 16
PLANES = 8
SLOTS = 32
PROWS = 128
RROWS = 256
SCALE = HD**-0.5 * 1.4426950408889634
LOW = -1e30
XS = 4
SENDS = 32
ARRIVALS = 78
COLS = 640
RA = 112
RB = RROWS - RA
HA, HB = 64, 80
ROLES = [(1, 2), (0, 2), (1, 1), (1, 3), (0, 1), (0, 3), (1, 0), (0, 0)]
MESH = pl.DeviceIdType.MESH


PLAN = [
    ([(0, 1, 0, 0), (0, -1, 0, 0)], 0, [(0, 2), (1, 0), (-1, 0)], [[]]),
    ([(0, 0, 1, 0), (1, 1, 0, 0), (1, 1, 0, 1), (0, 2, 0, 0), (0, -2, 0, 0)], 0, [(0, 1), (1, 2), (-1, 2), (0, 3), (2, 0), (-2, 0), (2, 2), (-2, 2)], [[(0, -1, 1, 0), (1, 1, 1, 0)]]),
    ([(1, 2, 0, 0), (1, 1, 1, 1), (0, 2, 1, 0), (0, 1, 1, 0), (1, 2, 0, 1)], 1, [(1, 0), (1, 2), (1, 1), (2, 0)], [[(0, 3, 0, 0)]]),
    ([(0, -2, 1, 0)], 0, [(-1, 1), (-1, 3), (2, 1), (1, 1), (2, 3), (1, 3), (3, 0), (-2, 1)], [[(1, 3, 0, 0)]]),
    ([(1, 2, 1, 0), (1, 3, 0, 1), (1, 2, 1, 1)], 1, [(1, 3), (2, 2), (3, 0), (2, 1)], [[(0, 4, 1, 0), (0, 3, 1, 0)]]),
    ([(1, 4, 0, 0), (0, 4, 0, 0), (1, 3, 1, 0), (1, 4, 0, 1)], 0, [(3, 2), (-2, 3), (4, 1), (3, 1), (4, 3), (3, 3), (4, 0), (4, 2)], [[(1, 3, 1, 1)]]),
    ([(0, 5, 1, 0)], 1, [(3, 2), (2, 3), (3, 1), (3, 3)], [[(0, 5, 0, 0)]]),
    ([(1, 4, 1, 0)], 0, [(5, 1), (5, 0), (5, 3), (5, 2)], [[]]),
    ([(1, 4, 1, 1)], 2, [], [[]]),
]

SPLIT = (2, 5)
DOWN, UP = 5, 2


def attend(q_ref, keys, values, bias_ref, top_ref, acc_ref, heads):
    count = keys.shape[0]
    widened = jnp.concatenate([values, jnp.ones((count, HD), jnp.bfloat16)], axis=1)
    for head in heads:
        scores = lax.dot_general(
            q_ref[:, head * HD : (head + 1) * HD],
            keys,
            (((1,), (1,)), ((), ())),
            preferred_element_type=jnp.float32,
        )
        if bias_ref is not None:
            scores = scores + bias_ref[:, :count]
        before = top_ref[head]
        top = jnp.maximum(before, jnp.max(scores, axis=1, keepdims=True) * SCALE)
        weights = jnp.exp2(scores * SCALE - top).astype(jnp.bfloat16)
        top_ref[head] = top
        acc_ref[head] = acc_ref[head] * jnp.exp2(before - top) + jnp.dot(
            weights, widened, preferred_element_type=jnp.float32
        )


def attention_block(
    lengths_hbm, q_hbm, pk_ref, pv_ref, rk_ref, rv_ref, w_ref, out_hbm,
    pbuf, rbuf, top_ref, acc_ref, bias_ref, first_ref, wbuf, att_ref, part,
    from_y, from_y_late, step1_r, step1_l, step2, late1_r, late1_l, late2,
    lengths_ref, q_ref, out_ref,
    load_sem, send_sem, recv_sem,
):
    s = lax.axis_index("seq")
    z, b = s // 4, s % 4
    h, c = b // 2, b % 2
    sibling = {"seq": z * 4 + h * 2 + (1 - c)}
    across = {"seq": z * 4 + (1 - h) * 2 + c}
    up = {"seq": ((z + 1) % PLANES) * 4 + b}
    up_two = {"seq": ((z + 2) % PLANES) * 4 + b}
    down_two = {"seq": ((z + PLANES - 2) % PLANES) * 4 + b}
    down = {"seq": ((z + PLANES - 1) % PLANES) * 4 + b}
    t = lax.axis_index("tp")
    yl, x = t // XS, t % XS
    right = {"tp": yl * XS + (x + 1) % XS}
    left = {"tp": yl * XS + (x + XS - 1) % XS}
    beside = {"tp": (1 - yl) * XS + x}
    order = [h * 2 + c, (1 - h) * 2 + c, h * 2 + (1 - c), (1 - h) * 2 + (1 - c)]

    loads = []
    for n, (src, dst) in enumerate(
        [
            (pk_ref, pbuf.at[s, 0]),
            (pv_ref, pbuf.at[s, 1]),
            (rk_ref, rbuf.at[s, 0]),
            (rv_ref, rbuf.at[s, 1]),
            (lengths_hbm, lengths_ref),
            (q_hbm, q_ref),
            (w_ref, wbuf),
        ]
    ):
        loads.append(pltpu.make_async_copy(src, dst, load_sem.at[n]))
        loads[-1].start()

    barrier = pltpu.get_barrier_semaphore()
    for peer in (sibling, across, up, down, right, left, beside, up_two, down_two):
        pl.semaphore_signal(barrier, inc=1, device_id=peer, device_id_type=MESH)

    def slot_of(kind, away, which):
        plane = (z + (PLANES - away if kind else PLANES + away)) % PLANES
        return plane * 4 + order[which]

    names = {}

    def name_of(*what):
        return names.setdefault(what, len(names))

    sends = []

    def start(src, dst, name, peer, only=None):
        number = len(sends)
        if number >= SENDS:
            finish(sends[number - SENDS])
        sending = pltpu.make_async_remote_copy(
            src_ref=src,
            dst_ref=dst,
            send_sem=send_sem.at[number % SENDS],
            recv_sem=recv_sem.at[name],
            device_id=peer,
            device_id_type=MESH,
        )
        sends.append((sending, only))
        if only is None:
            sending.start()
        else:
            pl.when(only)(sending.start)
        return sending

    def finish(entry):
        sending, only = entry
        if only is None:
            sending.wait_send()
        else:
            pl.when(only)(sending.wait_send)

    def part_of(kind, slot, piece):
        buf = rbuf if kind else pbuf
        return buf.at[slot] if piece == 2 else buf.at[slot, piece]

    def pass_on(kind, away, which, piece):
        slot = slot_of(kind, away, which)
        ref = part_of(kind, slot, piece)
        only = None
        if kind == 0:
            if which == 0:
                if away == 0:
                    start(ref, ref, name_of(0, 0, 1, 2), across)
                if 0 <= away < DOWN:
                    start(ref, ref, name_of(0, away + 1, 0, 2), down)
            elif away >= 0 and away % 2 == 0:
                if away + 2 <= DOWN:
                    start(ref, ref, name_of(0, away + 2, 1, 2), down_two)
                if away + 1 <= DOWN:
                    start(ref, ref, name_of(0, away + 1, 1, 2), down)
            if -UP < away <= 0:
                start(ref, ref, name_of(0, away - 1, which, 2), up)
        elif which == 0:
            if away < 4:
                start(ref, ref, name_of(1, away + 1, 0, piece), up)
            start(ref, ref, name_of(1, away, 1, piece), across, {0: h == 0, 4: h == 1}.get(away))
        else:
            only = {0: h == 1, 4: h == 0}.get(away)
        if piece > 0:
            ref = part_of(kind, slot, 2)
            start(ref, ref, name_of(kind, away, which + 2, 2), sibling, only)

    taken = {(0, 0, 0, 2), (1, 0, 0, 0), (1, 0, 0, 1)}

    def take(kind, away, which, piece):
        piece = piece if kind and which < 2 else 2
        if (kind, away, which, piece) in taken:
            return
        if piece == 1:
            take(kind, away, which, 0)
        taken.add((kind, away, which, piece))
        ref = part_of(kind, slot_of(kind, away, which), piece)
        number = name_of(kind, away, which, piece)
        arriving = pltpu.make_async_remote_copy(
            src_ref=ref,
            dst_ref=ref,
            send_sem=send_sem.at[0],
            recv_sem=recv_sem.at[number],
            device_id=sibling,
            device_id_type=MESH,
        )
        only = {0: h == 1, 4: h == 0}.get(away) if kind and which % 2 else None
        if only is None:
            arriving.wait_recv()
        else:
            pl.when(only)(arriving.wait_recv)
        if which < 2:
            pass_on(kind, away, which, piece)

    def visible(slot, at):
        position = s * RROWS + lax.broadcasted_iota(jnp.int32, (RROWS, 1), 0)
        key = slot * RROWS + lax.broadcasted_iota(jnp.int32, (RROWS, RROWS), 1)
        seen = (key >= first_ref[...]) & (key <= position)
        bias_ref[:, at : at + RROWS] = jnp.where(seen, 0.0, LOW)

    loads[4].wait()
    position = s * RROWS + lax.broadcasted_iota(jnp.int32, (RROWS, 1), 0)
    first = jnp.zeros((RROWS, 1), jnp.int32)
    begin = jnp.int32(0)
    for r in range(N_RESP):
        first = jnp.where(position >= begin, begin, first)
        begin = begin + lengths_ref[r]
    first_ref[...] = first
    top_ref[...] = jnp.full_like(top_ref, LOW)
    acc_ref[...] = jnp.zeros_like(acc_ref)
    for copying in loads[:4]:
        copying.wait()
    pl.semaphore_wait(barrier, 9)
    pass_on(0, 0, 0, 2)
    pass_on(1, 0, 0, 0)
    pass_on(1, 0, 0, 1)
    bias_ref[:, :PROWS] = jnp.zeros((RROWS, PROWS), jnp.float32)
    visible(s, PROWS)
    loads[5].wait()
    keys, values = [jnp.concatenate([pbuf[s, n], rbuf[s, n]], axis=0) for n in range(2)]
    attend(q_ref, keys, values, bias_ref, top_ref, acc_ref, range(GROUP))

    for step, (before, kind, shards, between) in enumerate(PLAN):
        for piece in before:
            take(*piece)
        if step == 1:
            take(1, 0, 1, 0)
            take(1, 0, 1, 1)
        for away, which in shards:
            for piece in range(kind + 1):
                take(kind, away, which, piece)
        if kind < 2:
            chosen = [slot_of(kind, *shard) for shard in shards]
        else:
            for away in (0, 4):
                for which in range(4):
                    take(1, away, which, 0)
                    take(1, away, which, 1)
            near = [slot_of(1, 0, which) for which in range(4)]
            far = [slot_of(1, 4, which) for which in range(4)]
            chosen = [far[0], c * near[2] + (1 - c) * far[2]] + [h * near[n] + (1 - h) * far[n] for n in (1, 3)]
        buf = rbuf if kind else pbuf
        if kind:
            for n, slot in enumerate(chosen):
                visible(slot, n * RROWS)
        keys, values = [jnp.concatenate([buf[slot, n] for slot in chosen], axis=0) for n in range(2)]
        edges = (0,) + SPLIT
        for n in range(len(SPLIT)):
            attend(q_ref, keys, values, bias_ref if kind else None, top_ref, acc_ref, range(edges[n], edges[n + 1]))
            if n < len(between):
                for piece in between[n]:
                    take(*piece)

    for head in range(GROUP):
        acc = acc_ref[head]
        att_ref[:, head * HD : (head + 1) * HD] = (acc[:, :HD] / acc[:, HD:]).astype(jnp.bfloat16)

    loads[6].wait()

    def hand(src, dst, peer):
        return start(src, dst, name_of(len(names)), peer)

    def compute(role):
        other, dx = ROLES[role]
        target = ((1 - yl) if other else yl) * XS + (x + dx) % XS
        columns = pl.ds(pl.multiple_of(target * COLS, HD), COLS)
        part[role] = jnp.dot(att_ref[...], wbuf[:, columns], preferred_element_type=jnp.float32).astype(jnp.bfloat16)

    def add(role, rows, *others):
        total = part[role, rows].astype(jnp.float32)
        for other in others:
            total = total + other.astype(jnp.float32)
        part[role, rows] = total.astype(jnp.bfloat16)

    rows_a, rows_b = slice(0, RA), slice(RA, RROWS)
    high_a, low_a = slice(0, HA), slice(HA, RA)
    high_b, low_b = slice(RA, RA + HB), slice(RA + HB, RROWS)
    ya, b1, b2 = {}, {}, {}
    compute(0)
    ya[0] = hand(part.at[0, rows_a], from_y.at[0], beside)
    b1[0, 0] = hand(part.at[0, high_b], step1_r.at[0], right)
    b1[1, 0] = hand(part.at[0, low_b], step1_l.at[0], left)
    compute(1)
    b1[0, 1] = hand(part.at[1, high_b], step1_r.at[1], right)
    b1[1, 1] = hand(part.at[1, low_b], step1_l.at[1], left)
    compute(2)
    ya[1] = hand(part.at[2, rows_a], from_y.at[1], beside)
    compute(3)
    ya[2] = hand(part.at[3, rows_a], from_y.at[2], beside)
    compute(6)
    ya[3] = hand(part.at[6, rows_a], from_y.at[3], beside)
    compute(4)
    compute(5)
    ya[0].wait_recv()
    add(1, rows_a, from_y[0])
    a1 = [hand(part.at[1, high_a], late1_r, right), hand(part.at[1, low_a], late1_l, left)]
    for n, (to_right, to_left) in enumerate([(2, 3), (4, 5)]):
        b1[0, n].wait_recv()
        add(to_right, high_b, step1_r[n])
        b2[0, n] = hand(part.at[to_right, rows_b], step2.at[0, n], right)
        b1[1, n].wait_recv()
        add(to_left, low_b, step1_l[n])
        b2[1, n] = hand(part.at[to_left, rows_b], step2.at[1, n], left)
    compute(7)
    a2 = []
    for n in range(2):
        ya[1 + n].wait_recv()
        add(4 + n, rows_a, from_y[1 + n])
        a1[n].wait_recv()
        add(4 + n, low_a if n else high_a, (late1_l if n else late1_r)[...])
        a2.append(hand(part.at[4 + n, rows_a], late2.at[n], left if n else right))
    for n in range(2):
        b2[n, 0].wait_recv()
    add(6, rows_b, step2[0, 0], step2[1, 0])
    yb = hand(part.at[6, rows_b], from_y_late, beside)
    ya[3].wait_recv()
    for n in range(2):
        a2[n].wait_recv()

    def total(rows, *others):
        result = part[7, rows].astype(jnp.float32)
        for other in others:
            result = result + other.astype(jnp.float32)
        out_ref[rows, :] = result.astype(jnp.bfloat16)

    total(rows_a, from_y[3], late2[0], late2[1])
    stores = [pltpu.make_async_copy(out_ref.at[rows], out_hbm.at[rows], load_sem.at[n]) for n, rows in enumerate((rows_a, rows_b))]
    stores[0].start()
    for n in range(2):
        b2[n, 1].wait_recv()
    yb.wait_recv()
    total(rows_b, step2[0, 1], step2[1, 1], from_y_late[...])
    stores[1].start()
    for entry in sends[-SENDS:]:
        finish(entry)
    for storing in stores:
        storing.wait()
    assert len(names) <= ARRIVALS


def per_device(queries, prompt_keys, prompt_values, response_keys, response_values, lengths, out_weight):
    anywhere = pl.BlockSpec(memory_space=pl.ANY)
    return pl.pallas_call(
        attention_block,
        out_shape=jax.ShapeDtypeStruct((RROWS, COLS), jnp.bfloat16),
        in_specs=[anywhere] * 7,
        out_specs=anywhere,
        scratch_shapes=[
            pltpu.VMEM((SLOTS, 2, PROWS, HD), jnp.bfloat16),
            pltpu.VMEM((SLOTS, 2, RROWS, HD), jnp.bfloat16),
            pltpu.VMEM((GROUP, RROWS, 1), jnp.float32),
            pltpu.VMEM((GROUP, RROWS, 2 * HD), jnp.float32),
            pltpu.VMEM((RROWS, 4 * RROWS), jnp.float32),
            pltpu.VMEM((RROWS, 1), jnp.int32),
            pltpu.VMEM(out_weight.shape, jnp.bfloat16),
            pltpu.VMEM((RROWS, GROUP * HD), jnp.bfloat16),
            pltpu.VMEM((8, RROWS, COLS), jnp.bfloat16),
            pltpu.VMEM((4, RA, COLS), jnp.bfloat16),
            pltpu.VMEM((RB, COLS), jnp.bfloat16),
            pltpu.VMEM((2, HB, COLS), jnp.bfloat16),
            pltpu.VMEM((2, RB - HB, COLS), jnp.bfloat16),
            pltpu.VMEM((2, 2, RB, COLS), jnp.bfloat16),
            pltpu.VMEM((HA, COLS), jnp.bfloat16),
            pltpu.VMEM((RA - HA, COLS), jnp.bfloat16),
            pltpu.VMEM((2, RA, COLS), jnp.bfloat16),
            pltpu.SMEM((N_RESP,), jnp.int32),
            pltpu.VMEM((RROWS, GROUP * HD), jnp.bfloat16),
            pltpu.VMEM((RROWS, COLS), jnp.bfloat16),
            pltpu.SemaphoreType.DMA((7,)),
            pltpu.SemaphoreType.DMA((SENDS,)),
            pltpu.SemaphoreType.DMA((ARRIVALS,)),
        ],
        compiler_params=pltpu.CompilerParams(
            collective_id=0, has_side_effects=True, vmem_limit_bytes=60 * 2**20
        ),
        name="attention_block",
    )(lengths, queries, prompt_keys, prompt_values, response_keys, response_values, out_weight)


def solution(mesh):
    in_specs = (P("seq", "tp"), P("seq", "tp"), P("seq", "tp"), P("seq", "tp"), P("seq", "tp"), P(), P("tp", None))
    return jax.shard_map(
        per_device, mesh=mesh, in_specs=in_specs, out_specs=P("seq", "tp"), check_vma=False
    )
```

```python
import functools

import jax
import jax.numpy as jnp
from jax import lax
from jax.experimental import pallas as pl
from jax.experimental.pallas import tpu as pltpu
from jax.sharding import PartitionSpec as P

HEADS = 40
KVH = 8
HD = 128
GROUP = HEADS // KVH
N_RESP = 16
PLANES = 8
SLOTS = 32
PROWS = 128
RROWS = 256
SCALE = HD**-0.5 * 1.4426950408889634
LOW = -1e30
XS = 4
SENDS = 32
ARRIVALS = 78
COLS = 640
RA = 112
RB = RROWS - RA
HA, HB = 64, 80
ROLES = [(1, 2), (0, 2), (1, 1), (1, 3), (0, 1), (0, 3), (1, 0), (0, 0)]
MESH = pl.DeviceIdType.MESH


PLAN = [
    ([(1, 1, 0, 0), (0, 1, 0, 0), (0, 0, 1, 0), (1, 1, 0, 1), (0, -1, 0, 0), (0, 2, 0, 0)], 0, [(0, 2), (1, 0), (0, 1), (1, 2), (0, 3), (-1, 0), (2, 0), (-1, 2)], []),
    ([(1, 2, 0, 0), (1, 1, 1, 0), (0, -1, 1, 0), (1, 1, 1, 1), (1, 2, 0, 1)], 1, [(1, 0), (1, 2), (1, 1), (2, 0)], []),
    ([(0, 2, 1, 0), (0, 1, 1, 0), (0, -2, 0, 0), (0, 3, 0, 0), (1, 3, 0, 0)], 0, [(2, 2), (-1, 1), (-1, 3), (2, 1), (1, 1), (-2, 0), (3, 0), (2, 3)], []),
    ([(1, 2, 1, 0), (0, -2, 1, 0), (1, 2, 1, 1), (1, 3, 0, 1)], 1, [(1, 3), (2, 2), (2, 1), (3, 0)], []),
    ([(0, -3, 0, 0), (1, 3, 1, 0), (0, 4, 1, 0), (0, 3, 1, 0)], 0, [(1, 3), (-2, 2), (3, 2), (-2, 1), (-2, 3), (-3, 0), (4, 1), (3, 1)], []),
    ([(1, 4, 0, 0), (0, 4, 0, 0), (0, -3, 1, 0), (1, 3, 1, 1), (1, 4, 0, 1)], 0, [(-3, 2), (4, 3), (3, 3), (4, 0), (-3, 1), (4, 2), (-3, 3)], []),
    ([], 1, [(2, 3), (3, 2), (3, 1), (3, 3)], []),
    ([(1, 4, 1, 0), (1, 4, 1, 1)], 2, [], []),
]
SPLIT = (5,)
DOWN, UP = 4, 3


def attend(q_ref, keys, values, bias_ref, top_ref, acc_ref, heads):
    count = keys.shape[0]
    widened = jnp.concatenate([values, jnp.ones((count, HD), jnp.bfloat16)], axis=1)
    for head in heads:
        scores = lax.dot_general(
            q_ref[:, head * HD : (head + 1) * HD],
            keys,
            (((1,), (1,)), ((), ())),
            preferred_element_type=jnp.float32,
        )
        if bias_ref is not None:
            scores = scores + bias_ref[:, :count]
        before = top_ref[head]
        top = jnp.maximum(before, jnp.max(scores, axis=1, keepdims=True) * SCALE)
        weights = jnp.exp2(scores * SCALE - top).astype(jnp.bfloat16)
        top_ref[head] = top
        acc_ref[head] = acc_ref[head] * jnp.exp2(before - top) + jnp.dot(
            weights, widened, preferred_element_type=jnp.float32
        )


def attention_block(
    lengths_hbm, q_hbm, pk_ref, pv_ref, rk_ref, rv_ref, w_ref, out_hbm,
    pbuf, rbuf, top_ref, acc_ref, bias_ref, first_ref, wbuf, att_ref, part,
    from_y, from_y_late, step1_r, step1_l, step2, late1_r, late1_l, late2,
    lengths_ref, q_ref, out_ref,
    load_sem, send_sem, recv_sem,
):
    s = lax.axis_index("seq")
    z, b = s // 4, s % 4
    h, c = b // 2, b % 2
    sibling = {"seq": z * 4 + h * 2 + (1 - c)}
    across = {"seq": z * 4 + (1 - h) * 2 + c}
    up = {"seq": ((z + 1) % PLANES) * 4 + b}
    up_two = {"seq": ((z + 2) % PLANES) * 4 + b}
    down_two = {"seq": ((z + PLANES - 2) % PLANES) * 4 + b}
    down = {"seq": ((z + PLANES - 1) % PLANES) * 4 + b}
    t = lax.axis_index("tp")
    yl, x = t // XS, t % XS
    right = {"tp": yl * XS + (x + 1) % XS}
    left = {"tp": yl * XS + (x + XS - 1) % XS}
    beside = {"tp": (1 - yl) * XS + x}
    order = [h * 2 + c, (1 - h) * 2 + c, h * 2 + (1 - c), (1 - h) * 2 + (1 - c)]

    loads = []
    for n, (src, dst) in enumerate(
        [
            (pk_ref, pbuf.at[s, 0]),
            (pv_ref, pbuf.at[s, 1]),
            (rk_ref, rbuf.at[s, 0]),
            (rv_ref, rbuf.at[s, 1]),
            (lengths_hbm, lengths_ref),
            (q_hbm, q_ref),
            (w_ref, wbuf),
        ]
    ):
        loads.append(pltpu.make_async_copy(src, dst, load_sem.at[n]))
        loads[-1].start()

    barrier = pltpu.get_barrier_semaphore()
    for peer in (sibling, across, up, down, right, left, beside, up_two, down_two):
        pl.semaphore_signal(barrier, inc=1, device_id=peer, device_id_type=MESH)

    def slot_of(kind, away, which):
        plane = (z + (PLANES - away if kind else PLANES + away)) % PLANES
        return plane * 4 + order[which]

    names = {}

    def name_of(*what):
        return names.setdefault(what, len(names))

    sends = []

    def start(src, dst, name, peer, only=None):
        number = len(sends)
        if number >= SENDS:
            finish(sends[number - SENDS])
        sending = pltpu.make_async_remote_copy(
            src_ref=src,
            dst_ref=dst,
            send_sem=send_sem.at[number % SENDS],
            recv_sem=recv_sem.at[name],
            device_id=peer,
            device_id_type=MESH,
        )
        sends.append((sending, only))
        if only is None:
            sending.start()
        else:
            pl.when(only)(sending.start)
        return sending

    def finish(entry):
        sending, only = entry
        if only is None:
            sending.wait_send()
        else:
            pl.when(only)(sending.wait_send)

    def part_of(kind, slot, piece):
        buf = rbuf if kind else pbuf
        return buf.at[slot] if piece == 2 else buf.at[slot, piece]

    def pass_on(kind, away, which, piece):
        slot = slot_of(kind, away, which)
        ref = part_of(kind, slot, piece)
        only = None
        if kind == 0:
            if which == 0:
                if away == 0:
                    start(ref, ref, name_of(0, 0, 1, 2), across)
                if 0 <= away < DOWN:
                    start(ref, ref, name_of(0, away + 1, 0, 2), down)
            elif away >= 0 and away % 2 == 0:
                if away + 2 <= DOWN:
                    start(ref, ref, name_of(0, away + 2, 1, 2), down_two)
                if away + 1 <= DOWN:
                    start(ref, ref, name_of(0, away + 1, 1, 2), down)
            if -UP < away <= 0:
                start(ref, ref, name_of(0, away - 1, which, 2), up)
        elif which == 0:
            if away < 4:
                start(ref, ref, name_of(1, away + 1, 0, piece), up)
            start(ref, ref, name_of(1, away, 1, piece), across, {0: h == 0, 4: h == 1}.get(away))
        else:
            only = {0: h == 1, 4: h == 0}.get(away)
        if piece > 0:
            ref = part_of(kind, slot, 2)
            start(ref, ref, name_of(kind, away, which + 2, 2), sibling, only)

    taken = {(0, 0, 0, 2), (1, 0, 0, 0), (1, 0, 0, 1)}

    def take(kind, away, which, piece):
        piece = piece if kind and which < 2 else 2
        if (kind, away, which, piece) in taken:
            return
        if piece == 1:
            take(kind, away, which, 0)
        taken.add((kind, away, which, piece))
        ref = part_of(kind, slot_of(kind, away, which), piece)
        number = name_of(kind, away, which, piece)
        arriving = pltpu.make_async_remote_copy(
            src_ref=ref,
            dst_ref=ref,
            send_sem=send_sem.at[0],
            recv_sem=recv_sem.at[number],
            device_id=sibling,
            device_id_type=MESH,
        )
        only = {0: h == 1, 4: h == 0}.get(away) if kind and which % 2 else None
        if only is None:
            arriving.wait_recv()
        else:
            pl.when(only)(arriving.wait_recv)
        if which < 2:
            pass_on(kind, away, which, piece)

    def visible(slot, at):
        position = s * RROWS + lax.broadcasted_iota(jnp.int32, (RROWS, 1), 0)
        key = slot * RROWS + lax.broadcasted_iota(jnp.int32, (RROWS, RROWS), 1)
        seen = (key >= first_ref[...]) & (key <= position)
        bias_ref[:, at : at + RROWS] = jnp.where(seen, 0.0, LOW)

    loads[4].wait()
    position = s * RROWS + lax.broadcasted_iota(jnp.int32, (RROWS, 1), 0)
    first = jnp.zeros((RROWS, 1), jnp.int32)
    begin = jnp.int32(0)
    for r in range(N_RESP):
        first = jnp.where(position >= begin, begin, first)
        begin = begin + lengths_ref[r]
    first_ref[...] = first
    top_ref[...] = jnp.full_like(top_ref, LOW)
    acc_ref[...] = jnp.zeros_like(acc_ref)
    for copying in loads[:4]:
        copying.wait()
    pl.semaphore_wait(barrier, 9)
    pass_on(0, 0, 0, 2)
    pass_on(1, 0, 0, 0)
    pass_on(1, 0, 0, 1)
    bias_ref[:, :PROWS] = jnp.zeros((RROWS, PROWS), jnp.float32)
    visible(s, PROWS)
    loads[5].wait()
    keys, values = [jnp.concatenate([pbuf[s, n], rbuf[s, n]], axis=0) for n in range(2)]
    attend(q_ref, keys, values, bias_ref, top_ref, acc_ref, range(GROUP))

    for step, (before, kind, shards, between) in enumerate(PLAN):
        for piece in before:
            take(*piece)
        if step == 1:
            take(1, 0, 1, 0)
            take(1, 0, 1, 1)
        for away, which in shards:
            for piece in range(kind + 1):
                take(kind, away, which, piece)
        if kind < 2:
            chosen = [slot_of(kind, *shard) for shard in shards]
        else:
            for away in (0, 4):
                for which in range(4):
                    take(1, away, which, 0)
                    take(1, away, which, 1)
            near = [slot_of(1, 0, which) for which in range(4)]
            far = [slot_of(1, 4, which) for which in range(4)]
            chosen = [far[0], c * near[2] + (1 - c) * far[2]] + [h * near[n] + (1 - h) * far[n] for n in (1, 3)]
        buf = rbuf if kind else pbuf
        if kind:
            for n, slot in enumerate(chosen):
                visible(slot, n * RROWS)
        keys, values = [jnp.concatenate([buf[slot, n] for slot in chosen], axis=0) for n in range(2)]
        edges = (0,) + SPLIT
        for n in range(len(SPLIT)):
            attend(q_ref, keys, values, bias_ref if kind else None, top_ref, acc_ref, range(edges[n], edges[n + 1]))
            if n < len(between):
                for piece in between[n]:
                    take(*piece)

    for head in range(GROUP):
        acc = acc_ref[head]
        att_ref[:, head * HD : (head + 1) * HD] = (acc[:, :HD] / acc[:, HD:]).astype(jnp.bfloat16)

    loads[6].wait()

    def hand(src, dst, peer):
        return start(src, dst, name_of(len(names)), peer)

    def compute(role):
        other, dx = ROLES[role]
        target = ((1 - yl) if other else yl) * XS + (x + dx) % XS
        columns = pl.ds(pl.multiple_of(target * COLS, HD), COLS)
        part[role] = jnp.dot(att_ref[...], wbuf[:, columns], preferred_element_type=jnp.float32).astype(jnp.bfloat16)

    def add(role, rows, *others):
        total = part[role, rows].astype(jnp.float32)
        for other in others:
            total = total + other.astype(jnp.float32)
        part[role, rows] = total.astype(jnp.bfloat16)

    rows_a, rows_b = slice(0, RA), slice(RA, RROWS)
    high_a, low_a = slice(0, HA), slice(HA, RA)
    high_b, low_b = slice(RA, RA + HB), slice(RA + HB, RROWS)
    ya, b1, b2 = {}, {}, {}
    compute(0)
    ya[0] = hand(part.at[0, rows_a], from_y.at[0], beside)
    b1[0, 0] = hand(part.at[0, high_b], step1_r.at[0], right)
    b1[1, 0] = hand(part.at[0, low_b], step1_l.at[0], left)
    compute(1)
    b1[0, 1] = hand(part.at[1, high_b], step1_r.at[1], right)
    b1[1, 1] = hand(part.at[1, low_b], step1_l.at[1], left)
    compute(2)
    ya[1] = hand(part.at[2, rows_a], from_y.at[1], beside)
    compute(3)
    ya[2] = hand(part.at[3, rows_a], from_y.at[2], beside)
    compute(6)
    ya[3] = hand(part.at[6, rows_a], from_y.at[3], beside)
    compute(4)
    compute(5)
    ya[0].wait_recv()
    add(1, rows_a, from_y[0])
    a1 = [hand(part.at[1, high_a], late1_r, right), hand(part.at[1, low_a], late1_l, left)]
    for n, (to_right, to_left) in enumerate([(2, 3), (4, 5)]):
        b1[0, n].wait_recv()
        add(to_right, high_b, step1_r[n])
        b2[0, n] = hand(part.at[to_right, rows_b], step2.at[0, n], right)
        b1[1, n].wait_recv()
        add(to_left, low_b, step1_l[n])
        b2[1, n] = hand(part.at[to_left, rows_b], step2.at[1, n], left)
    compute(7)
    a2 = []
    for n in range(2):
        ya[1 + n].wait_recv()
        add(4 + n, rows_a, from_y[1 + n])
        a1[n].wait_recv()
        add(4 + n, low_a if n else high_a, (late1_l if n else late1_r)[...])
        a2.append(hand(part.at[4 + n, rows_a], late2.at[n], left if n else right))
    for n in range(2):
        b2[n, 0].wait_recv()
    add(6, rows_b, step2[0, 0], step2[1, 0])
    yb = hand(part.at[6, rows_b], from_y_late, beside)
    ya[3].wait_recv()
    for n in range(2):
        a2[n].wait_recv()

    def total(rows, *others):
        result = part[7, rows].astype(jnp.float32)
        for other in others:
            result = result + other.astype(jnp.float32)
        out_ref[rows, :] = result.astype(jnp.bfloat16)

    total(rows_a, from_y[3], late2[0], late2[1])
    stores = [pltpu.make_async_copy(out_ref.at[rows], out_hbm.at[rows], load_sem.at[n]) for n, rows in enumerate((rows_a, rows_b))]
    stores[0].start()
    for n in range(2):
        b2[n, 1].wait_recv()
    yb.wait_recv()
    total(rows_b, step2[0, 1], step2[1, 1], from_y_late[...])
    stores[1].start()
    for entry in sends[-SENDS:]:
        finish(entry)
    for storing in stores:
        storing.wait()
    assert len(names) <= ARRIVALS


def per_device(queries, prompt_keys, prompt_values, response_keys, response_values, lengths, out_weight):
    anywhere = pl.BlockSpec(memory_space=pl.ANY)
    return pl.pallas_call(
        attention_block,
        out_shape=jax.ShapeDtypeStruct((RROWS, COLS), jnp.bfloat16),
        in_specs=[anywhere] * 7,
        out_specs=anywhere,
        scratch_shapes=[
            pltpu.VMEM((SLOTS, 2, PROWS, HD), jnp.bfloat16),
            pltpu.VMEM((SLOTS, 2, RROWS, HD), jnp.bfloat16),
            pltpu.VMEM((GROUP, RROWS, 1), jnp.float32),
            pltpu.VMEM((GROUP, RROWS, 2 * HD), jnp.float32),
            pltpu.VMEM((RROWS, 4 * RROWS), jnp.float32),
            pltpu.VMEM((RROWS, 1), jnp.int32),
            pltpu.VMEM(out_weight.shape, jnp.bfloat16),
            pltpu.VMEM((RROWS, GROUP * HD), jnp.bfloat16),
            pltpu.VMEM((8, RROWS, COLS), jnp.bfloat16),
            pltpu.VMEM((4, RA, COLS), jnp.bfloat16),
            pltpu.VMEM((RB, COLS), jnp.bfloat16),
            pltpu.VMEM((2, HB, COLS), jnp.bfloat16),
            pltpu.VMEM((2, RB - HB, COLS), jnp.bfloat16),
            pltpu.VMEM((2, 2, RB, COLS), jnp.bfloat16),
            pltpu.VMEM((HA, COLS), jnp.bfloat16),
            pltpu.VMEM((RA - HA, COLS), jnp.bfloat16),
            pltpu.VMEM((2, RA, COLS), jnp.bfloat16),
            pltpu.SMEM((N_RESP,), jnp.int32),
            pltpu.VMEM((RROWS, GROUP * HD), jnp.bfloat16),
            pltpu.VMEM((RROWS, COLS), jnp.bfloat16),
            pltpu.SemaphoreType.DMA((7,)),
            pltpu.SemaphoreType.DMA((SENDS,)),
            pltpu.SemaphoreType.DMA((ARRIVALS,)),
        ],
        compiler_params=pltpu.CompilerParams(
            collective_id=0, has_side_effects=True, vmem_limit_bytes=60 * 2**20
        ),
        name="attention_block",
    )(lengths, queries, prompt_keys, prompt_values, response_keys, response_values, out_weight)


def solution(mesh):
    in_specs = (P("seq", "tp"), P("seq", "tp"), P("seq", "tp"), P("seq", "tp"), P("seq", "tp"), P(), P("tp", None))
    return jax.shard_map(
        per_device, mesh=mesh, in_specs=in_specs, out_specs=P("seq", "tp"), check_vma=False
    )
```

```python
import functools

import jax
import jax.numpy as jnp
from jax import lax
from jax.experimental import pallas as pl
from jax.experimental.pallas import tpu as pltpu
from jax.sharding import PartitionSpec as P

HEADS = 40
KVH = 8
HD = 128
GROUP = HEADS // KVH
N_RESP = 16
PLANES = 8
SLOTS = 32
PROWS = 128
RROWS = 256
SCALE = HD**-0.5 * 1.4426950408889634
LOW = -1e30
XS = 4
SENDS = 32
ARRIVALS = 78
COLS = 640
RA = 112
RB = RROWS - RA
HA, HB = 64, 80
ROLES = [(1, 2), (0, 2), (1, 1), (1, 3), (0, 1), (0, 3), (1, 0), (0, 0)]
MESH = pl.DeviceIdType.MESH


PLAN = [
    ([(1, 1, 0, 0), (0, 1, 0, 0), (0, 0, 1, 0), (1, 1, 0, 1), (0, -1, 0, 0), (0, 2, 0, 0)], 0, [(0, 2), (1, 0), (0, 1), (1, 2), (0, 3), (-1, 0), (2, 0), (-1, 2)], []),
    ([(1, 2, 0, 0), (1, 1, 1, 0), (0, -1, 1, 0), (1, 1, 1, 1), (1, 2, 0, 1)], 1, [(1, 0), (1, 2), (1, 1), (2, 0)], []),
    ([(0, 2, 1, 0), (0, 1, 1, 0), (0, -2, 0, 0), (0, 3, 0, 0), (1, 3, 0, 0)], 0, [(2, 2), (-1, 1), (-1, 3), (2, 1), (1, 1), (-2, 0), (3, 0), (2, 3)], []),
    ([(1, 2, 1, 0), (0, -2, 1, 0), (1, 2, 1, 1), (1, 3, 0, 1)], 1, [(1, 3), (2, 2), (2, 1), (3, 0)], []),
    ([(0, -3, 0, 0), (1, 3, 1, 0), (0, 4, 1, 0), (0, 3, 1, 0)], 0, [(1, 3), (-2, 2), (3, 2), (-2, 1), (-2, 3), (-3, 0), (4, 1), (3, 1)], []),
    ([(1, 4, 0, 0), (0, 4, 0, 0), (0, -3, 1, 0), (1, 3, 1, 1), (1, 4, 0, 1)], 0, [(-3, 2), (4, 3), (3, 3), (4, 0), (-3, 1), (4, 2), (-3, 3)], []),
    ([], 1, [(2, 3), (3, 2), (3, 1), (3, 3)], []),
    ([(1, 4, 1, 0), (1, 4, 1, 1)], 2, [], []),
]
SPLIT = (5,)
DOWN, UP = 4, 3


def attend(q_ref, keys, values, bias_ref, top_ref, acc_ref, heads):
    count = keys.shape[0]
    widened = jnp.concatenate([values, jnp.ones((count, HD), jnp.bfloat16)], axis=1)
    for head in heads:
        scores = lax.dot_general(
            q_ref[:, head * HD : (head + 1) * HD],
            keys,
            (((1,), (1,)), ((), ())),
            preferred_element_type=jnp.float32,
        )
        if bias_ref is not None:
            scores = scores + bias_ref[:, :count]
        before = top_ref[head]
        top = jnp.maximum(before, jnp.max(scores, axis=1, keepdims=True) * SCALE)
        weights = jnp.exp2(scores * SCALE - top).astype(jnp.bfloat16)
        top_ref[head] = top
        acc_ref[head] = acc_ref[head] * jnp.exp2(before - top) + jnp.dot(
            weights, widened, preferred_element_type=jnp.float32
        )


def attention_block(
    lengths_hbm, q_hbm, pk_ref, pv_ref, rk_ref, rv_ref, w_ref, out_hbm,
    pbuf, rbuf, top_ref, acc_ref, bias_ref, first_ref, wbuf, att_ref, part,
    from_y, from_y_late, step1_r, step1_l, step2, late1_r, late1_l, late2,
    lengths_ref, q_ref, out_ref,
    load_sem, send_sem, recv_sem,
):
    s = lax.axis_index("seq")
    z, b = s // 4, s % 4
    h, c = b // 2, b % 2
    sibling = {"seq": z * 4 + h * 2 + (1 - c)}
    across = {"seq": z * 4 + (1 - h) * 2 + c}
    up = {"seq": ((z + 1) % PLANES) * 4 + b}
    up_two = {"seq": ((z + 2) % PLANES) * 4 + b}
    down_two = {"seq": ((z + PLANES - 2) % PLANES) * 4 + b}
    down = {"seq": ((z + PLANES - 1) % PLANES) * 4 + b}
    t = lax.axis_index("tp")
    yl, x = t // XS, t % XS
    right = {"tp": yl * XS + (x + 1) % XS}
    left = {"tp": yl * XS + (x + XS - 1) % XS}
    beside = {"tp": (1 - yl) * XS + x}
    order = [h * 2 + c, (1 - h) * 2 + c, h * 2 + (1 - c), (1 - h) * 2 + (1 - c)]

    loads = []
    for n, (src, dst) in enumerate(
        [
            (pk_ref, pbuf.at[s, 0]),
            (pv_ref, pbuf.at[s, 1]),
            (rk_ref, rbuf.at[s, 0]),
            (rv_ref, rbuf.at[s, 1]),
            (lengths_hbm, lengths_ref),
            (q_hbm, q_ref),
            (w_ref, wbuf),
        ]
    ):
        loads.append(pltpu.make_async_copy(src, dst, load_sem.at[n]))
        loads[-1].start()

    barrier = pltpu.get_barrier_semaphore()
    for peer in (sibling, across, up, down, right, left, beside, up_two, down_two):
        pl.semaphore_signal(barrier, inc=1, device_id=peer, device_id_type=MESH)

    def slot_of(kind, away, which):
        plane = (z + (PLANES - away if kind else PLANES + away)) % PLANES
        return plane * 4 + order[which]

    names = {}

    def name_of(*what):
        return names.setdefault(what, len(names))

    sends = []

    def start(src, dst, name, peer, only=None):
        number = len(sends)
        if number >= SENDS:
            finish(sends[number - SENDS])
        sending = pltpu.make_async_remote_copy(
            src_ref=src,
            dst_ref=dst,
            send_sem=send_sem.at[number % SENDS],
            recv_sem=recv_sem.at[name],
            device_id=peer,
            device_id_type=MESH,
        )
        sends.append((sending, only))
        if only is None:
            sending.start()
        else:
            pl.when(only)(sending.start)
        return sending

    def finish(entry):
        sending, only = entry
        if only is None:
            sending.wait_send()
        else:
            pl.when(only)(sending.wait_send)

    def part_of(kind, slot, piece):
        buf = rbuf if kind else pbuf
        return buf.at[slot] if piece == 2 else buf.at[slot, piece]

    def pass_on(kind, away, which, piece):
        slot = slot_of(kind, away, which)
        ref = part_of(kind, slot, piece)
        only = None
        if kind == 0:
            if which == 0:
                if away == 0:
                    start(ref, ref, name_of(0, 0, 1, 2), across)
                if 0 <= away < DOWN:
                    start(ref, ref, name_of(0, away + 1, 0, 2), down)
            elif away >= 0 and away % 2 == 0:
                if away + 2 <= DOWN:
                    start(ref, ref, name_of(0, away + 2, 1, 2), down_two)
                if away + 1 <= DOWN:
                    start(ref, ref, name_of(0, away + 1, 1, 2), down)
            if -UP < away <= 0:
                start(ref, ref, name_of(0, away - 1, which, 2), up)
        elif which == 0:
            if away < 4:
                start(ref, ref, name_of(1, away + 1, 0, piece), up)
            start(ref, ref, name_of(1, away, 1, piece), across, {0: h == 0, 4: h == 1}.get(away))
        else:
            only = {0: h == 1, 4: h == 0}.get(away)
        if piece > 0:
            ref = part_of(kind, slot, 2)
            start(ref, ref, name_of(kind, away, which + 2, 2), sibling, only)

    taken = {(0, 0, 0, 2), (1, 0, 0, 0), (1, 0, 0, 1)}

    def take(kind, away, which, piece):
        piece = piece if kind and which < 2 else 2
        if (kind, away, which, piece) in taken:
            return
        if piece == 1:
            take(kind, away, which, 0)
        taken.add((kind, away, which, piece))
        ref = part_of(kind, slot_of(kind, away, which), piece)
        number = name_of(kind, away, which, piece)
        arriving = pltpu.make_async_remote_copy(
            src_ref=ref,
            dst_ref=ref,
            send_sem=send_sem.at[0],
            recv_sem=recv_sem.at[number],
            device_id=sibling,
            device_id_type=MESH,
        )
        only = {0: h == 1, 4: h == 0}.get(away) if kind and which % 2 else None
        if only is None:
            arriving.wait_recv()
        else:
            pl.when(only)(arriving.wait_recv)
        if which < 2:
            pass_on(kind, away, which, piece)

    def visible(slot, at):
        position = s * RROWS + lax.broadcasted_iota(jnp.int32, (RROWS, 1), 0)
        key = slot * RROWS + lax.broadcasted_iota(jnp.int32, (RROWS, RROWS), 1)
        seen = (key >= first_ref[...]) & (key <= position)
        bias_ref[:, at : at + RROWS] = jnp.where(seen, 0.0, LOW)

    loads[4].wait()
    position = s * RROWS + lax.broadcasted_iota(jnp.int32, (RROWS, 1), 0)
    first = jnp.zeros((RROWS, 1), jnp.int32)
    begin = jnp.int32(0)
    for r in range(N_RESP):
        first = jnp.where(position >= begin, begin, first)
        begin = begin + lengths_ref[r]
    first_ref[...] = first
    top_ref[...] = jnp.full_like(top_ref, LOW)
    acc_ref[...] = jnp.zeros_like(acc_ref)
    for copying in loads[:4]:
        copying.wait()
    pl.semaphore_wait(barrier, 9)
    pass_on(0, 0, 0, 2)
    pass_on(1, 0, 0, 0)
    pass_on(1, 0, 0, 1)
    bias_ref[:, :PROWS] = jnp.zeros((RROWS, PROWS), jnp.float32)
    visible(s, PROWS)
    loads[5].wait()
    keys, values = [jnp.concatenate([pbuf[s, n], rbuf[s, n]], axis=0) for n in range(2)]
    attend(q_ref, keys, values, bias_ref, top_ref, acc_ref, range(GROUP))

    for step, (before, kind, shards, between) in enumerate(PLAN):
        for piece in before:
            take(*piece)
        if step == 1:
            take(1, 0, 1, 0)
            take(1, 0, 1, 1)
        for away, which in shards:
            for piece in range(kind + 1):
                take(kind, away, which, piece)
        if kind < 2:
            chosen = [slot_of(kind, *shard) for shard in shards]
        else:
            for away in (0, 4):
                for which in range(4):
                    take(1, away, which, 0)
                    take(1, away, which, 1)
            near = [slot_of(1, 0, which) for which in range(4)]
            far = [slot_of(1, 4, which) for which in range(4)]
            chosen = [far[0], c * near[2] + (1 - c) * far[2]] + [h * near[n] + (1 - h) * far[n] for n in (1, 3)]
        buf = rbuf if kind else pbuf
        if kind:
            for n, slot in enumerate(chosen):
                visible(slot, n * RROWS)
        keys, values = [jnp.concatenate([buf[slot, n] for slot in chosen], axis=0) for n in range(2)]
        edges = (0,) + SPLIT
        for n in range(len(SPLIT)):
            attend(q_ref, keys, values, bias_ref if kind else None, top_ref, acc_ref, range(edges[n], edges[n + 1]))
            if n < len(between):
                for piece in between[n]:
                    take(*piece)

    for head in range(GROUP):
        acc = acc_ref[head]
        att_ref[:, head * HD : (head + 1) * HD] = (acc[:, :HD] / acc[:, HD:]).astype(jnp.bfloat16)

    loads[6].wait()

    def hand(src, dst, peer):
        return start(src, dst, name_of(len(names)), peer)

    def compute(role):
        other, dx = ROLES[role]
        target = ((1 - yl) if other else yl) * XS + (x + dx) % XS
        columns = pl.ds(pl.multiple_of(target * COLS, HD), COLS)
        part[role] = jnp.dot(att_ref[...], wbuf[:, columns], preferred_element_type=jnp.float32).astype(jnp.bfloat16)

    def add(role, rows, *others):
        total = part[role, rows].astype(jnp.float32)
        for other in others:
            total = total + other.astype(jnp.float32)
        part[role, rows] = total.astype(jnp.bfloat16)

    rows_a, rows_b = slice(0, RA), slice(RA, RROWS)
    high_a, low_a = slice(0, HA), slice(HA, RA)
    high_b, low_b = slice(RA, RA + HB), slice(RA + HB, RROWS)
    ya, b1, b2 = {}, {}, {}
    compute(0)
    ya[0] = hand(part.at[0, rows_a], from_y.at[0], beside)
    b1[0, 0] = hand(part.at[0, high_b], step1_r.at[0], right)
    b1[1, 0] = hand(part.at[0, low_b], step1_l.at[0], left)
    compute(1)
    b1[0, 1] = hand(part.at[1, high_b], step1_r.at[1], right)
    b1[1, 1] = hand(part.at[1, low_b], step1_l.at[1], left)
    compute(2)
    ya[1] = hand(part.at[2, rows_a], from_y.at[1], beside)
    compute(3)
    ya[2] = hand(part.at[3, rows_a], from_y.at[2], beside)
    compute(6)
    ya[3] = hand(part.at[6, rows_a], from_y.at[3], beside)
    compute(4)
    compute(5)
    a1 = []
    for n, (to_right, to_left) in enumerate([(2, 3), (4, 5)]):
        if n:
            ya[0].wait_recv()
            add(1, rows_a, from_y[0])
            a1 += [hand(part.at[1, high_a], late1_r, right), hand(part.at[1, low_a], late1_l, left)]
        b1[0, n].wait_recv()
        add(to_right, high_b, step1_r[n])
        b2[0, n] = hand(part.at[to_right, rows_b], step2.at[0, n], right)
        b1[1, n].wait_recv()
        add(to_left, low_b, step1_l[n])
        b2[1, n] = hand(part.at[to_left, rows_b], step2.at[1, n], left)
    compute(7)
    a2 = []
    for n in range(2):
        ya[1 + n].wait_recv()
        add(4 + n, rows_a, from_y[1 + n])
        a1[n].wait_recv()
        add(4 + n, low_a if n else high_a, (late1_l if n else late1_r)[...])
        a2.append(hand(part.at[4 + n, rows_a], late2.at[n], left if n else right))
    for n in range(2):
        b2[n, 0].wait_recv()
    add(6, rows_b, step2[0, 0], step2[1, 0])
    yb = hand(part.at[6, rows_b], from_y_late, beside)
    ya[3].wait_recv()
    for n in range(2):
        a2[n].wait_recv()

    def total(rows, *others):
        result = part[7, rows].astype(jnp.float32)
        for other in others:
            result = result + other.astype(jnp.float32)
        out_ref[rows, :] = result.astype(jnp.bfloat16)

    total(rows_a, from_y[3], late2[0], late2[1])
    stores = [pltpu.make_async_copy(out_ref.at[rows], out_hbm.at[rows], load_sem.at[n]) for n, rows in enumerate((rows_a, rows_b))]
    stores[0].start()
    for n in range(2):
        b2[n, 1].wait_recv()
    yb.wait_recv()
    total(rows_b, step2[0, 1], step2[1, 1], from_y_late[...])
    stores[1].start()
    for entry in sends[-SENDS:]:
        finish(entry)
    for storing in stores:
        storing.wait()
    assert len(names) <= ARRIVALS


def per_device(queries, prompt_keys, prompt_values, response_keys, response_values, lengths, out_weight):
    anywhere = pl.BlockSpec(memory_space=pl.ANY)
    return pl.pallas_call(
        attention_block,
        out_shape=jax.ShapeDtypeStruct((RROWS, COLS), jnp.bfloat16),
        in_specs=[anywhere] * 7,
        out_specs=anywhere,
        scratch_shapes=[
            pltpu.VMEM((SLOTS, 2, PROWS, HD), jnp.bfloat16),
            pltpu.VMEM((SLOTS, 2, RROWS, HD), jnp.bfloat16),
            pltpu.VMEM((GROUP, RROWS, 1), jnp.float32),
            pltpu.VMEM((GROUP, RROWS, 2 * HD), jnp.float32),
            pltpu.VMEM((RROWS, 4 * RROWS), jnp.float32),
            pltpu.VMEM((RROWS, 1), jnp.int32),
            pltpu.VMEM(out_weight.shape, jnp.bfloat16),
            pltpu.VMEM((RROWS, GROUP * HD), jnp.bfloat16),
            pltpu.VMEM((8, RROWS, COLS), jnp.bfloat16),
            pltpu.VMEM((4, RA, COLS), jnp.bfloat16),
            pltpu.VMEM((RB, COLS), jnp.bfloat16),
            pltpu.VMEM((2, HB, COLS), jnp.bfloat16),
            pltpu.VMEM((2, RB - HB, COLS), jnp.bfloat16),
            pltpu.VMEM((2, 2, RB, COLS), jnp.bfloat16),
            pltpu.VMEM((HA, COLS), jnp.bfloat16),
            pltpu.VMEM((RA - HA, COLS), jnp.bfloat16),
            pltpu.VMEM((2, RA, COLS), jnp.bfloat16),
            pltpu.SMEM((N_RESP,), jnp.int32),
            pltpu.VMEM((RROWS, GROUP * HD), jnp.bfloat16),
            pltpu.VMEM((RROWS, COLS), jnp.bfloat16),
            pltpu.SemaphoreType.DMA((7,)),
            pltpu.SemaphoreType.DMA((SENDS,)),
            pltpu.SemaphoreType.DMA((ARRIVALS,)),
        ],
        compiler_params=pltpu.CompilerParams(
            collective_id=0, has_side_effects=True, vmem_limit_bytes=60 * 2**20
        ),
        name="attention_block",
    )(lengths, queries, prompt_keys, prompt_values, response_keys, response_values, out_weight)


def solution(mesh):
    in_specs = (P("seq", "tp"), P("seq", "tp"), P("seq", "tp"), P("seq", "tp"), P("seq", "tp"), P(), P("tp", None))
    return jax.shard_map(
        per_device, mesh=mesh, in_specs=in_specs, out_specs=P("seq", "tp"), check_vma=False
    )
```
